32 devices in a mesh: row: 4 (over y, x), col: 8 (over z, core).
Axes of the slice: x: 2, y: 2, z: 4, core: 2. Of those that a mesh axis runs over, the one named last changes fastest.
Arguments:
- integrals: bfloat16 [2880, 23040], P('row', 'col'), may hold values from -0.0390625 to 0.0390625
- amplitudes: bfloat16 [23040, 256], P('col', 'row'), may hold values from -6 to 6
Outputs:
- ladder: bfloat16 [256, 2880], P('col', 'row')
The draws below stay inside these ranges and needn't reach their ends.
All inputs are finite; a program needn't handle non-finite values.
Results may differ from the reference program's by a relative error of at most 0.001.
Values may be sent and summed in bfloat16 or wider, within the bound.
A program may use at most 64 MiB of HBM per device.

```python
import jax
import jax.numpy as jnp
from jax import lax

AB = 2880
CD = 23040
PAIRS = 256


def steps_of(key, shape, pieces, least, largest):
    level, own = 1.0, jax.random.fold_in(key, 6)
    for axis_at, blocks in pieces:
        steps = jnp.exp(jax.random.uniform(jax.random.fold_in(own, axis_at), (blocks,), jnp.float32, least / len(pieces), largest / len(pieces)))
        level = level * jnp.repeat(steps, shape[axis_at] // blocks).reshape([-1 if axis == axis_at else 1 for axis in range(len(shape))])
    return level


def noise(own_key, dims, spread, most, pieces=(), held_as=jnp.bfloat16):
    entries = spread * jax.random.normal(own_key, dims, jnp.float32)
    if pieces:
        entries = entries * steps_of(own_key, dims, pieces, -0.22, 0.18)
    return jnp.clip(entries, -most, most).astype(held_as)


def setup_inputs(seed: int = 0) -> dict:
    splits = jax.random.split(jax.random.key(seed), 3)
    integrals = noise(splits[0], (AB, CD), CD ** -0.5, 0.0390625, ((0, 4), (1, 8)))
    amplitudes = noise(splits[1], (CD, PAIRS), 1.0, 6.0, ((0, 8), (1, 4)))
    return {"integrals": integrals, "amplitudes": amplitudes}


def reference(integrals, amplitudes):
    ladder_sum = lax.dot_general(amplitudes, integrals, (((0,), (1,)), ((), ())), preferred_element_type=jnp.float32)
    return ladder_sum.astype(jnp.bfloat16)
```

```python
import functools

import jax
import jax.numpy as jnp
from jax import lax
from jax.experimental import pallas as pl
from jax.experimental.pallas import tpu as pltpu
from jax.sharding import PartitionSpec as P

MESH = pl.DeviceIdType.MESH
NT = (((1,), (1,)), ((), ()))
SLOTS = 6
A1, A2, L1, L2, R1, R2 = range(6)


def cuts_of(size, pieces, step):
    width = -(-size // (pieces * step)) * step
    return [(at, min(width, size - at)) for at in range(0, size, width)]


def ladder_kernel(chips, cuts, v_ref, t_ref, out_ref, v, t, o_parts, o_swap, o_sum, parts, swap, summed, landed,
                  v_sem, t_sem, sent, came, swap_send, swap_recv, line_send, line_recv, known):
    pairs = t_ref.shape[0]
    q = pairs // 4
    r, c = lax.axis_index("row"), lax.axis_index("col")
    z, core = c // 2, c % 2
    rx = r + 1 - 2 * (r % 2)
    ry = r + 2 - 4 * (r // 2)
    rd = 3 - r
    partner = 2 * z + 1 - core
    above, below = z < chips - 1, z > 0
    x_own_last = (r // 2) == (z // 2)
    y_own_last = (r % 2) == (z % 2)

    t_copy = pltpu.make_async_copy(t_ref, t.at[pl.ds(0, pairs)], t_sem)
    t_copy.start()
    v_copies = []
    for i, (at, width) in enumerate(cuts):
        copy = pltpu.make_async_copy(v_ref.at[:, pl.ds(at, width)], v.at[:, pl.ds(at, width)], v_sem.at[i])
        copy.start()
        v_copies.append(copy)

    barrier = pltpu.get_barrier_semaphore()

    def signal(sem, **to):
        pl.semaphore_signal(sem, inc=1, device_id=to, device_id_type=MESH)

    def signal_line(up, down):
        @pl.when(above)
        def _():
            signal(up, col=c + 2)

        @pl.when(below)
        def _():
            signal(down, col=c - 2)

    signal(barrier, row=rx)
    signal(barrier, row=ry)
    signal(barrier, col=partner)
    signal_line(barrier, barrier)
    pl.semaphore_wait(barrier, 5 - jnp.where(above, 0, 1) - jnp.where(below, 0, 1))

    lies = ([pairs, pairs + q, pairs + 2 * q, pairs + 3 * q, 3 * pairs + 2 * q, 3 * pairs + 3 * q],
            [2 * pairs + 2 * q, 2 * pairs + 3 * q, 2 * pairs, 2 * pairs + q, 3 * pairs, 3 * pairs + q])
    own_rows = ([0, q, 2 * q, 3 * q], [2 * q, 3 * q, 0, q])
    to_row = (rx, ry)

    def item_copies(link, item):
        copies = []
        whole = [(0, t_ref.shape[1])] if item < L2 else cuts
        for n, (at, width) in enumerate(whole):
            columns = pl.ds(at, width)
            if item <= L2:
                source = t_ref.at[pl.ds(own_rows[link][item], q), columns]
            else:
                source = t.at[pl.ds(lies[1 - link][item - R1], q), columns]
            copies.append(pltpu.make_async_remote_copy(
                src_ref=source, dst_ref=t.at[pl.ds(lies[link][item], q), columns],
                send_sem=sent.at[link, item, n], recv_sem=came.at[link, item, n],
                device_id={"row": to_row[link]}, device_id_type=MESH))
        return copies

    items = [[item_copies(link, item) for item in range(6)] for link in range(2)]

    def start(link, item):
        for copy in items[link][item]:
            copy.start()

    for item in (A1, A2, L1):
        for link in range(2):
            start(link, item)
    own_last = (x_own_last, y_own_last)
    for link in range(2):
        @pl.when(jnp.logical_not(own_last[link]))
        def _():
            start(link, L2)
    signal_line(known.at[0], known.at[1])

    def heard(first, second):
        @pl.when(below)
        def _():
            pl.semaphore_wait(known.at[first], 1)

        @pl.when(above)
        def _():
            pl.semaphore_wait(known.at[second], 1)

    def slot_items(s):
        if s < 3:
            return [s, s]
        last, early = ((R1, L2), (R2, R1), (L2, R2))[s - 3]
        return [jnp.where(own_last[link], last, early) for link in range(2)]

    def pick(table, item):
        if isinstance(item, int):
            return table[item]
        at = table[-1]
        for n in range(len(table) - 2, L2 - 1, -1):
            at = jnp.where(item == n, table[n], at)
        return pl.multiple_of(at, q)

    def arrive(s, n):
        for link, item in enumerate(slot_items(s)):
            rows = t.at[pl.ds(pick(lies[link], item), q)]
            if n is None:
                held = rows
                pltpu.make_async_copy(held, held, came.at[link, item, 0]).wait()
            else:
                at, width = cuts[n]
                held = rows.at[:, pl.ds(at, width)]
                pltpu.make_async_copy(held, held, came.at[link, item, n]).wait()

    def low_link(s):
        return 0 if s < 2 else 1

    def multiply(s, at, width):
        found = slot_items(s)
        low = low_link(s)
        rows = [t[pl.ds(pick(lies[link], found[link]), q), at:at + width] for link in (low, 1 - low)]
        return lax.dot_general(
            jnp.concatenate(rows, axis=0), v[:, at:at + width], NT, preferred_element_type=jnp.float32)

    def kept(s):
        found = slot_items(s)
        low = low_link(s)
        beside = (rx, ry)

        def goal(link):
            if isinstance(found[link], int):
                return beside[link]
            return jnp.where(found[link] >= R1, rd, beside[link])

        def place(link):
            return (found[link] % 2) * q

        where = jnp.where(core == 0, goal(low), goal(1 - low))
        spot = jnp.where(core == 0, place(low), place(1 - low))
        return where, pl.multiple_of(spot, q)

    def swap_copy(s):
        if s is None:
            source, target, n = o_parts.at[1 - core], o_swap, SLOTS
        else:
            source, target, n = parts.at[s, 1 - core], swap.at[s], s
        return pltpu.make_async_remote_copy(
            src_ref=source, dst_ref=target, send_sem=swap_send.at[n], recv_sem=swap_recv.at[n],
            device_id={"col": partner}, device_id_type=MESH)

    def line_copy(s):
        if s is None:
            source, rows, n, goal = o_sum, pl.ds(0, 2 * q), SLOTS, r
        else:
            goal, spot = kept(s)
            source, rows, n = summed.at[s], pl.ds(spot, q), s
        return pltpu.make_async_remote_copy(
            src_ref=source, dst_ref=landed.at[z, rows], send_sem=line_send.at[n], recv_sem=line_recv.at[z],
            device_id={"col": 2 * goal + core}, device_id_type=MESH), goal, rows

    def swap_finish(s):
        swap_copy(s).wait_recv()
        if s is None:
            total = o_parts[core] + o_swap[...]
        else:
            total = parts[s, core] + swap[s]
        copy, goal, rows = line_copy(s)

        @pl.when(goal == z)
        def _():
            landed[z, rows] = total

        @pl.when(goal != z)
        def _():
            if s is None:
                o_sum[...] = total
            else:
                summed[s] = total
            copy.start()

    def store(s, value):
        parts[s, 0] = value[:q]
        parts[s, 1] = value[q:]
        swap_copy(s).start()

    t_copy.wait()
    total = None
    for i, (at, width) in enumerate(cuts):
        v_copies[i].wait()
        term = lax.dot_general(
            t[:pairs, at:at + width], v[:, at:at + width], NT, preferred_element_type=jnp.float32)
        total = term if total is None else total + term
    o_parts[0] = total[:2 * q]
    o_parts[1] = total[2 * q:]
    swap_copy(None).start()
    heard(0, 1)
    signal_line(known.at[2], known.at[3])
    heard(2, 3)
    swap_finish(None)

    for s in range(SLOTS - 1):
        if s < 3:
            arrive(s, None)
        else:
            for n in range(len(cuts)):
                arrive(s, n)
        if s < 2:
            for link in range(2):
                start(link, (R1, R2)[s])
        if s == 1:
            for link in range(2):
                @pl.when(own_last[link])
                def _():
                    start(link, L2)
        store(s, multiply(s, 0, t_ref.shape[1]))
        if s > 0:
            swap_finish(s - 1)

    s = SLOTS - 1
    total = None
    for n, (at, width) in enumerate(cuts):
        arrive(s, n)
        term = multiply(s, at, width)
        total = term if total is None else total + term
        if n == 0:
            swap_finish(s - 1)
    store(s, total)
    swap_finish(s)

    for source in range(chips):
        @pl.when(z != source)
        def _():
            pltpu.make_async_copy(landed.at[source], landed.at[source], line_recv.at[source]).wait()
    total = landed[0]
    for source in range(1, chips):
        total = total + landed[source]
    out_ref[...] = total.astype(out_ref.dtype)

    for link in range(2):
        for item in range(6):
            for copy in items[link][item]:
                copy.wait_send()
    for s in [None, *range(SLOTS)]:
        swap_copy(s).wait_send()
        copy, goal, _ = line_copy(s)

        @pl.when(goal != z)
        def _():
            copy.wait_send()


def ladder_on_chips(integrals, amplitudes):
    chips = lax.axis_size("col") // 2
    blocks = amplitudes.T
    pairs, depth = blocks.shape
    rows = integrals.shape[0]
    q = pairs // 4
    cuts = cuts_of(depth, 4, 256)
    f32 = jnp.float32
    dma = pltpu.SemaphoreType.DMA
    return pl.pallas_call(
        functools.partial(ladder_kernel, chips, cuts),
        out_shape=jax.ShapeDtypeStruct((2 * q, rows), jnp.bfloat16),
        in_specs=[pl.BlockSpec(memory_space=pl.ANY)] * 2,
        out_specs=pl.BlockSpec(memory_space=pltpu.VMEM),
        scratch_shapes=[
            pltpu.VMEM((rows, depth), jnp.bfloat16),
            pltpu.VMEM((4 * pairs, depth), jnp.bfloat16),
            pltpu.VMEM((2, 2 * q, rows), f32),
            pltpu.VMEM((2 * q, rows), f32),
            pltpu.VMEM((2 * q, rows), f32),
            pltpu.VMEM((SLOTS, 2, q, rows), f32),
            pltpu.VMEM((SLOTS, q, rows), f32),
            pltpu.VMEM((SLOTS, q, rows), f32),
            pltpu.VMEM((chips, 2 * q, rows), f32),
            dma((len(cuts),)), dma,
            dma((2, 6, len(cuts))), dma((2, 6, len(cuts))),
            dma((SLOTS + 1,)), dma((SLOTS + 1,)),
            dma((SLOTS + 1,)), dma((chips,)),
            pltpu.SemaphoreType.REGULAR((4,)),
        ],
        compiler_params=pltpu.CompilerParams(
            collective_id=0, has_side_effects=True, vmem_limit_bytes=67043328),
    )(integrals, blocks)


def per_device(integrals, amplitudes):
    columns = lax.axis_size("col")
    if lax.axis_size("row") == 4 and columns == 8 and amplitudes.shape[1] % 64 == 0:
        return ladder_on_chips(integrals, amplitudes)
    gathered = lax.all_gather(amplitudes, "row", axis=1, tiled=True)
    product = lax.dot_general(
        gathered, integrals, (((0,), (1,)), ((), ())), preferred_element_type=jnp.float32)
    return lax.psum_scatter(product, "col", scatter_dimension=0, tiled=True).astype(jnp.bfloat16)


def solution(mesh):
    in_specs = (P("row", "col"), P("col", "row"))
    out_specs = P("col", "row")
    return jax.shard_map(
        per_device, mesh=mesh, in_specs=in_specs, out_specs=out_specs, check_vma=False
    )
```

```python
import functools

import jax
import jax.numpy as jnp
from jax import lax
from jax.experimental import pallas as pl
from jax.experimental.pallas import tpu as pltpu
from jax.sharding import PartitionSpec as P

MESH = pl.DeviceIdType.MESH
NT = (((1,), (1,)), ((), ()))


def cuts_of(size, pieces, step):
    width = -(-size // (pieces * step)) * step
    return [(at, min(width, size - at)) for at in range(0, size, width)]


def ladder_kernel(chips, cuts, v_ref, t_ref, out_ref, v, t, parts, swap, summed, landed,
                  v_sem, t_sem, near_send, near_recv, far_send, far_recv, late_send, late_recv, last_send, last_recv,
                  swap_send, swap_recv, line_send, line_recv, known):
    depth = t_ref.shape[1]
    half = t_ref.shape[0] // 2
    part = half // 2
    r, c = lax.axis_index("row"), lax.axis_index("col")
    z, core = c // 2, c % 2
    rx = r + 1 - 2 * (r % 2)
    ry = r + 2 - 4 * (r // 2)
    rd = 3 - r
    other = 1 - core
    own = (0, half, (r, r), 0)
    near = (2 * half, half, (rx, ry), 0)
    far = [(4 * half + 2 * part * j, part, (rd, rd), part * j) for j in range(2)]
    late = (6 * half, half, (ry, rx), 0)
    slots = [own, near, *far, late]

    t_copy = pltpu.make_async_copy(t_ref, t.at[pl.ds(0, 2 * half)], t_sem)
    t_copy.start()
    v_copies = []
    for i, (at, width) in enumerate(cuts):
        copy = pltpu.make_async_copy(v_ref.at[:, pl.ds(at, width)], v.at[:, pl.ds(at, width)], v_sem.at[i])
        copy.start()
        v_copies.append(copy)

    barrier = pltpu.get_barrier_semaphore()
    pl.semaphore_signal(barrier, inc=1, device_id={"row": rx}, device_id_type=MESH)
    pl.semaphore_signal(barrier, inc=1, device_id={"row": ry}, device_id_type=MESH)
    pl.semaphore_signal(barrier, inc=1, device_id={"col": 2 * z + other}, device_id_type=MESH)
    above, below = z < chips - 1, z > 0

    def signal_line(up, down):
        @pl.when(above)
        def _():
            pl.semaphore_signal(up, inc=1, device_id={"col": c + 2}, device_id_type=MESH)

        @pl.when(below)
        def _():
            pl.semaphore_signal(down, inc=1, device_id={"col": c - 2}, device_id_type=MESH)

    def heard(first, second):
        @pl.when(below)
        def _():
            pl.semaphore_wait(known.at[first], 1)

        @pl.when(above)
        def _():
            pl.semaphore_wait(known.at[second], 1)

    signal_line(barrier, barrier)
    pl.semaphore_wait(barrier, 5 - jnp.where(above, 0, 1) - jnp.where(below, 0, 1))
    signal_line(known.at[0], known.at[1])

    def send(source, target, to, sems):
        copy = pltpu.make_async_remote_copy(
            src_ref=source, dst_ref=target, send_sem=sems[0], recv_sem=sems[1],
            device_id={"row": to}, device_id_type=MESH)
        copy.start()
        return copy

    def at_rows(first, count):
        return t.at[pl.ds(first, count)]

    near_copies = []
    for j in range(2):
        for h, to in ((0, rx), (1, ry)):
            near_copies.append(send(
                t_ref.at[pl.ds(h * half + j * part, part)], at_rows(near[0] + h * half + j * part, part), to,
                (near_send.at[j, h], near_recv.at[j, h])))

    def relay(j):
        copies = []
        for h, to in ((0, ry), (1, rx)):
            copies.append(send(
                at_rows(near[0] + h * half + j * part, part), at_rows(far[j][0] + h * part, part), to,
                (far_send.at[j, h], far_recv.at[j, h])))
        return copies

    def multiply(slot, at, width):
        first, count = slot[0], 2 * slot[1]
        return lax.dot_general(
            t[first:first + count, at:at + width], v[:, at:at + width], NT, preferred_element_type=jnp.float32)

    def swap_start(i):
        first, count, _, _ = slots[i]
        copy = pltpu.make_async_remote_copy(
            src_ref=parts.at[pl.ds(first + other * count, count)], dst_ref=swap.at[pl.ds(first // 2, count)],
            send_sem=swap_send.at[i], recv_sem=swap_recv.at[i],
            device_id={"col": 2 * z + other}, device_id_type=MESH)
        copy.start()
        return copy

    def goal(i):
        one, two = slots[i][2]
        return one * other + two * core

    def line_copy(i):
        first, count, _, place = slots[i]
        return pltpu.make_async_remote_copy(
            src_ref=summed.at[pl.ds(first // 2, count)], dst_ref=landed.at[z, pl.ds(place, count)],
            send_sem=line_send.at[i], recv_sem=line_recv.at[z],
            device_id={"col": 2 * goal(i) + core}, device_id_type=MESH)

    def swap_finish(i, copy):
        first, count, _, place = slots[i]
        copy.wait_recv()
        total = parts[pl.ds(first + core * count, count)] + swap[first // 2:first // 2 + count]

        @pl.when(goal(i) == z)
        def _():
            landed[z, place:place + count] = total

        @pl.when(goal(i) != z)
        def _():
            summed[first // 2:first // 2 + count] = total
            line_copy(i).start()

    def store(i, value):
        first, count = slots[i][0], 2 * slots[i][1]
        parts[first:first + count] = value

    def wait(copies):
        for copy in copies:
            copy.wait_recv()

    t_copy.wait()
    total = None
    for i, (at, width) in enumerate(cuts):
        v_copies[i].wait()
        term = multiply(own, at, width)
        total = term if total is None else total + term
    store(0, total)
    swaps = [swap_start(0)]
    heard(0, 1)
    signal_line(known.at[2], known.at[3])
    heard(2, 3)

    wait(near_copies[:2])
    far_copies = relay(0)
    swap_finish(0, swaps[0])
    wait(near_copies[2:])
    far_copies += relay(1)
    late_copies = []
    for h, to in ((1, rx), (0, ry)):
        late_copies.append(send(
            t_ref.at[pl.ds(h * half, part)], at_rows(late[0] + h * half, part), to,
            (late_send.at[h], late_recv.at[h])))
    last_copies = []
    for i, (at, width) in enumerate(cuts):
        for h, to in ((1, rx), (0, ry)):
            last_copies.append(send(
                t_ref.at[pl.ds(h * half + part, part), pl.ds(at, width)],
                t.at[pl.ds(late[0] + h * half + part, part), pl.ds(at, width)], to,
                (last_send.at[i, h], last_recv.at[i, h])))
    store(1, multiply(near, 0, depth))
    swaps.append(swap_start(1))

    wait(far_copies[:2])
    store(2, multiply(far[0], 0, depth))
    swaps.append(swap_start(2))
    swap_finish(1, swaps[1])

    wait(far_copies[2:])
    store(3, multiply(far[1], 0, depth))
    swaps.append(swap_start(3))
    swap_finish(2, swaps[2])

    wait(late_copies)
    total = None
    for i, (at, width) in enumerate(cuts):
        wait(last_copies[2 * i:2 * i + 2])
        term = multiply(late, at, width)
        total = term if total is None else total + term
        if i == 0:
            swap_finish(3, swaps[3])
    store(4, total)
    swaps.append(swap_start(4))
    swap_finish(4, swaps[4])

    for source in range(chips):
        @pl.when(z != source)
        def _():
            pltpu.make_async_copy(landed.at[source], landed.at[source], line_recv.at[source]).wait()
    total = landed[0]
    for source in range(1, chips):
        total = total + landed[source]
    out_ref[...] = total.astype(out_ref.dtype)

    for copy in near_copies + far_copies + late_copies + last_copies + swaps:
        copy.wait_send()
    for i in range(len(slots)):
        @pl.when(goal(i) != z)
        def _():
            line_copy(i).wait_send()


def ladder_on_chips(integrals, amplitudes):
    chips = lax.axis_size("col") // 2
    blocks = amplitudes.T
    pairs, depth = blocks.shape
    rows = integrals.shape[0]
    half = pairs // 2
    cuts = cuts_of(depth, 2, 256)
    f32 = jnp.float32
    dma = pltpu.SemaphoreType.DMA
    return pl.pallas_call(
        functools.partial(ladder_kernel, chips, cuts),
        out_shape=jax.ShapeDtypeStruct((half, rows), jnp.bfloat16),
        in_specs=[pl.BlockSpec(memory_space=pl.ANY)] * 2,
        out_specs=pl.BlockSpec(memory_space=pltpu.VMEM),
        scratch_shapes=[
            pltpu.VMEM((rows, depth), jnp.bfloat16),
            pltpu.VMEM((4 * pairs, depth), jnp.bfloat16),
            pltpu.VMEM((4 * pairs, rows), f32),
            pltpu.VMEM((2 * pairs, rows), f32),
            pltpu.VMEM((2 * pairs, rows), f32),
            pltpu.VMEM((chips, half, rows), f32),
            dma((len(cuts),)), dma,
            dma((2, 2)), dma((2, 2)),
            dma((2, 2)), dma((2, 2)),
            dma((2,)), dma((2,)),
            dma((len(cuts), 2)), dma((len(cuts), 2)),
            dma((5,)), dma((5,)),
            dma((5,)), dma((chips,)),
            pltpu.SemaphoreType.REGULAR((4,)),
        ],
        compiler_params=pltpu.CompilerParams(
            collective_id=0, has_side_effects=True, vmem_limit_bytes=67043328),
    )(integrals, blocks)


def per_device(integrals, amplitudes):
    columns = lax.axis_size("col")
    if lax.axis_size("row") == 4 and columns == 8:
        return ladder_on_chips(integrals, amplitudes)
    gathered = lax.all_gather(amplitudes, "row", axis=1, tiled=True)
    product = lax.dot_general(
        gathered, integrals, (((0,), (1,)), ((), ())), preferred_element_type=jnp.float32)
    return lax.psum_scatter(product, "col", scatter_dimension=0, tiled=True).astype(jnp.bfloat16)


def solution(mesh):
    in_specs = (P("row", "col"), P("col", "row"))
    out_specs = P("col", "row")
    return jax.shard_map(
        per_device, mesh=mesh, in_specs=in_specs, out_specs=out_specs, check_vma=False
    )
```
